32 devices in a mesh: reg: 16 (over z, x, core), lev: 2 (over y).
Axes of the slice: x: 2, y: 2, z: 4, core: 2. Of those that a mesh axis runs over, the one named last changes fastest.
Arguments:
- state_now: bfloat16 [24, 1280, 2560], P(None, 'reg', 'lev'), may hold values from -6 to 6
- dep_cell: int32 [8, 1280, 2560], P(None, 'reg', 'lev'), may hold values from 0 to 63, as said below
- weight_code: int32 [8, 1280, 2560], P(None, 'reg', 'lev'), may hold values from 0 to 288, as said below
- wave_speed: float32 [8], replicated, may hold values from 0.05 to 5
Outputs:
- state_next: bfloat16 [24, 1280, 2560], P(None, 'reg', 'lev')
The draws below stay inside these ranges and needn't reach their ends.
Inputs may be any that keep to these rules, and one draw needn't show every extreme that they name: `dep_cell`: 2 * 4 (a + 4) + b + 4 with whole numbers a and b from -4 to 3; both ends of that range occur for a and for b. `weight_code`: 17 a + b with whole numbers a and b from 0 to 16.
All inputs are finite; a program needn't handle non-finite values.
Results may differ from the reference program's by a relative error of at most 0.0084.
Values may be sent and summed in bfloat16 or wider, within the bound.
A program may use at most 64 MiB of HBM per device.

```python
import math
import jax
import jax.numpy as jnp
from jax import lax

NLAT = 1280
NLON = 2560
MX = 640
MY = 640
LEVS = 8
FIELDS = 3
HALO = 4


def draw_dep_cell(key, part):
    key_rows, key_cols = jax.random.split(jax.random.fold_in(key, 11))
    shift_row = jax.random.randint(key_rows, (LEVS, NLAT, NLON), -HALO, HALO)
    shift_col = jax.random.randint(key_cols, (LEVS, NLAT, NLON), -HALO, HALO)
    shift_row = shift_row.at[0, 1, 1].set(-HALO).at[0, 2, 2].set(HALO - 1).at[0, 0, 0].set(-1).at[1, 0, 0].set(0)
    shift_col = shift_col.at[0, 1, 1].set(HALO - 1).at[0, 2, 2].set(-HALO).at[0, 0, 0].set(-1).at[1, 0, 0].set(0)
    shift_row = shift_row.at[0, 5, 5].set(HALO - 1).at[0, 6, 6].set(-HALO)
    shift_col = shift_col.at[0, 5, 5].set(HALO - 1).at[0, 6, 6].set(-HALO)
    return ((shift_row + HALO) * (2 * HALO) + (shift_col + HALO)).astype(jnp.int32)


def draw_weight_code(key, part):
    key_rows, key_cols = jax.random.split(jax.random.fold_in(key, 23))
    weight_row = jax.random.randint(key_rows, (LEVS, NLAT, NLON), 0, 17)
    weight_col = jax.random.randint(key_cols, (LEVS, NLAT, NLON), 0, 17)
    codes = 17 * weight_row + weight_col
    codes = codes.at[0, 3, 3].set(288).at[0, 4, 4].set(0)
    return codes.astype(jnp.int32)


def shard_levels(own_key, extent, cuts, low, top_value):
    factor_of, own = 1.0, jax.random.fold_in(own_key, 6)
    for dim, blocks in cuts:
        heights = jnp.exp(jax.random.uniform(jax.random.fold_in(own, dim), (blocks,), jnp.float32, low / len(cuts), top_value / len(cuts)))
        factor_of = factor_of * jnp.repeat(heights, extent[dim] // blocks).reshape([-1 if axis == dim else 1 for axis in range(len(extent))])
    return factor_of


def gaussian(own_key, shape, width, limit, cuts=(), held_as=jnp.bfloat16):
    result = width * jax.random.normal(own_key, shape, jnp.float32)
    if cuts:
        result = result * shard_levels(own_key, shape, cuts, -0.22, 0.18)
    return jnp.clip(result, -limit, limit).astype(held_as)


def setup_inputs(seed: int = 0) -> dict:
    keys = jax.random.split(jax.random.key(seed), 5)
    state_now = gaussian(keys[0], (FIELDS * LEVS, NLAT, NLON), 1.0, 6.0, ((1, 16), (2, 2)))
    dep_cell = draw_dep_cell(jax.random.fold_in(keys[4], 71), 0)
    weight_code = draw_weight_code(jax.random.fold_in(keys[4], 71), 0)
    wave_speed = jnp.clip(jnp.exp(jax.random.uniform(keys[3], (LEVS,), jnp.float32, math.log(0.05), math.log(5.0))), 0.05, 5.0)
    return dict(state_now=state_now, dep_cell=dep_cell, weight_code=weight_code, wave_speed=wave_speed)


def wave_table(length, modes, offset, amount):
    position = offset + lax.iota(jnp.int32, amount)
    wavenum = lax.iota(jnp.int32, 2 * modes) % modes
    product = (position[:, None] * wavenum[None, :]) % length
    angles = product.astype(jnp.float32) * (2.0 * math.pi / length)
    cosine_part = lax.iota(jnp.int32, 2 * modes) < modes
    return jnp.where(cosine_part[None, :], jnp.cos(angles), jnp.sin(angles)).astype(jnp.bfloat16)


def implicit_solve(spectral, xindex, speeds):
    wave_x = xindex % MX
    wave_y = lax.iota(jnp.int32, 2 * MY) % MY
    kx_term = (2.0 * math.pi / NLON) * wave_x.astype(jnp.float32)
    ky_term = (2.0 * math.pi / NLAT) * wave_y.astype(jnp.float32)
    laplace = kx_term[:, None] ** 2 + ky_term[None, :] ** 2
    inside = (wave_x[:, None] * wave_x[:, None] + wave_y[None, :] * wave_y[None, :] < MX * MY)
    weight_x = jnp.where(wave_x == 0, 1.0, 2.0)
    weight_y = jnp.where(wave_y == 0, 1.0, 2.0)
    factor = jnp.where(inside, weight_x[:, None] * weight_y[None, :], 0.0).astype(jnp.float32)
    speed_sq = speeds[:, None, None]
    vorticity = spectral[:, 0]
    divergence = spectral[:, 1]
    pressure = spectral[:, 2]
    div_new = (divergence + laplace * pressure) / (1.0 + speed_sq * laplace)
    pres_new = pressure - speed_sq * div_new
    stacked = jnp.stack([vorticity, div_new, pres_new], axis=1)
    return (stacked * factor[None, None]).astype(jnp.bfloat16)


def interpolate_level(inputs):
    field_data, cell_code, code_index = inputs
    flat_pos = lax.iota(jnp.int32, NLAT * NLON)
    row_arrive = flat_pos // NLON
    col_arrive = flat_pos % NLON
    shift_row = cell_code // (2 * HALO) - HALO
    shift_col = cell_code % (2 * HALO) - HALO
    row_index = (row_arrive + shift_row + NLAT) % NLAT
    col_index = (col_arrive + shift_col + NLON) % NLON
    row_next = (row_index + 1) % NLAT
    col_next = (col_index + 1) % NLON
    weight_row = (code_index // 17).astype(jnp.float32) / 16.0
    weight_col = (code_index % 17).astype(jnp.float32) / 16.0

    def sample(rows_at, cols_at):
        return field_data[:, rows_at * NLON + cols_at].astype(jnp.float32)

    blended = ((1.0 - weight_row) * (1.0 - weight_col) * sample(row_index, col_index)
               + (1.0 - weight_row) * weight_col * sample(row_index, col_next)
               + weight_row * (1.0 - weight_col) * sample(row_next, col_index)
               + weight_row * weight_col * sample(row_next, col_next))
    return blended.astype(jnp.bfloat16)


def reference(state_now, dep_cell, weight_code, wave_speed):
    stacked = FIELDS * LEVS
    upstream = lax.map(interpolate_level, (state_now.reshape(LEVS, FIELDS, NLAT * NLON),
                                           dep_cell.reshape(LEVS, NLAT * NLON),
                                           weight_code.reshape(LEVS, NLAT * NLON)))
    lon_table = wave_table(NLON, MX, 0, NLON)
    lat_table = wave_table(NLAT, MY, 0, NLAT)
    lon_sum = jnp.dot(upstream.reshape(stacked * NLAT, NLON), lon_table, preferred_element_type=jnp.float32)
    lon_coef = (lon_sum / NLON).astype(jnp.bfloat16).reshape(stacked, NLAT, 2 * MX)
    by_coef = lon_coef.transpose(0, 2, 1).reshape(stacked * 2 * MX, NLAT)
    spectral = jnp.dot(by_coef, lat_table, preferred_element_type=jnp.float32) / NLAT
    spectral = spectral.reshape(LEVS, FIELDS, 2 * MX, 2 * MY)
    solved = implicit_solve(spectral, lax.iota(jnp.int32, 2 * MX), wave_speed)
    back_lat = jnp.dot(solved.reshape(stacked * 2 * MX, 2 * MY), lat_table.T,
                       preferred_element_type=jnp.float32).astype(jnp.bfloat16)
    by_row = back_lat.reshape(stacked, 2 * MX, NLAT).transpose(0, 2, 1).reshape(stacked * NLAT, 2 * MX)
    state_next = jnp.dot(by_row, lon_table.T, preferred_element_type=jnp.float32).astype(jnp.bfloat16)
    return state_next.reshape(stacked, NLAT, NLON)
```

```python
import math

import jax
import jax.numpy as jnp
import ml_dtypes
import numpy as np
from jax import lax
from jax.experimental import pallas as pl
from jax.experimental.pallas import tpu as pltpu
from jax.sharding import PartitionSpec as P

NLAT = 1280
NLON = 2560
MX = 640
MY = 640
FIELDS = 3
HALO = 4
LANES = 128
ROWS = 16


def padded_2(block, sides, width):
    for axis, dim in sides:
        count = lax.axis_size(axis)
        forward = [(i, i + 1) for i in range(count - 1)]
        forward.append((count - 1, 0))
        backward = [(target, source) for source, target in forward]
        low = lax.ppermute(
            lax.slice_in_dim(block, block.shape[dim] - width, None, axis=dim), axis, forward
        )
        high = lax.ppermute(lax.slice_in_dim(block, 0, width, axis=dim), axis, backward)
        block = jnp.concatenate([low, block, high], axis=dim)
    return block


def wave_table(length, modes, offset, amount):
    position = offset + lax.iota(jnp.int32, amount)
    wavenum = lax.iota(jnp.int32, 2 * modes) % modes
    product = position[:, None] * wavenum[None, :] % length
    angles = product.astype(jnp.float32) * (2.0 * math.pi / length)
    cosine_part = lax.iota(jnp.int32, 2 * modes) < modes
    return jnp.where(cosine_part[None, :], jnp.cos(angles), jnp.sin(angles)).astype(jnp.bfloat16)


def implicit_solve(spectral, xindex, speeds):
    wave_x = xindex % MX
    wave_y = lax.iota(jnp.int32, 2 * MY) % MY
    kx_term = 2.0 * math.pi / NLON * wave_x.astype(jnp.float32)
    ky_term = 2.0 * math.pi / NLAT * wave_y.astype(jnp.float32)
    laplace = kx_term[:, None] ** 2 + ky_term[None, :] ** 2
    inside = wave_x[:, None] * wave_x[:, None] + wave_y[None, :] * wave_y[None, :] < MX * MY
    weight_x = jnp.where(wave_x == 0, 1.0, 2.0)
    weight_y = jnp.where(wave_y == 0, 1.0, 2.0)
    factor = jnp.where(inside, weight_x[:, None] * weight_y[None, :], 0.0).astype(jnp.float32)
    speed_sq = speeds[:, None, None]
    vorticity = spectral[:, 0]
    divergence = spectral[:, 1]
    pressure = spectral[:, 2]
    div_new = (divergence + laplace * pressure) / (1.0 + speed_sq * laplace)
    pres_new = pressure - speed_sq * div_new
    stacked = jnp.stack([vorticity, div_new, pres_new], axis=1)
    return (stacked * factor[None, None]).astype(jnp.bfloat16)


def shift_weights(cell_code, code_index):
    shift_row = cell_code // (2 * HALO) - HALO
    shift_col = cell_code % (2 * HALO) - HALO
    weight_row = (code_index // 17).astype(jnp.float32) / 16.0
    weight_col = (code_index % 17).astype(jnp.float32) / 16.0
    row_weights = []
    col_weights = []
    for offset in range(-HALO, HALO + 1):
        row_weights.append(
            jnp.where(shift_row == offset, 1.0 - weight_row, 0.0)
            + jnp.where(shift_row + 1 == offset, weight_row, 0.0)
        )
        col_weights.append(
            jnp.where(shift_col == offset, 1.0 - weight_col, 0.0)
            + jnp.where(shift_col + 1 == offset, weight_col, 0.0)
        )
    return (row_weights, col_weights)


def interpolate_local(padded, row_weights, col_weights):
    levels, rows_pad, cols_pad = padded.shape
    rows_here = rows_pad - 2 * HALO
    cols_here = cols_pad - 2 * HALO
    blended = jnp.zeros((levels, rows_here, cols_here), jnp.float32)
    for row_step in range(2 * HALO + 1):
        inner = jnp.zeros((levels, rows_here, cols_here), jnp.float32)
        for col_step in range(2 * HALO + 1):
            window = padded[:, row_step : row_step + rows_here, col_step : col_step + cols_here]
            inner = inner + col_weights[col_step] * window.astype(jnp.float32)
        blended = blended + row_weights[row_step] * inner
    return blended.astype(jnp.bfloat16)


def per_device(state_now, dep_cell, weight_code, wave_speed):
    stacked, rows_here, cols_here = state_now.shape
    levels = stacked // FIELDS
    col_first = lax.axis_index("lev") * cols_here
    grouped = state_now.reshape(levels, FIELDS, rows_here, cols_here)
    row_weights, col_weights = shift_weights(dep_cell, weight_code)
    passes = []
    for which_field in range(FIELDS):
        padded = padded_2(grouped[:, which_field], (("reg", 1), ("lev", 2)), HALO)
        passes.append(interpolate_local(padded, row_weights, col_weights))
    upstream = jnp.stack(passes, axis=1).reshape(stacked, rows_here, cols_here)
    lon_table = wave_table(NLON, MX, 0, NLON)
    full_rows = lax.all_to_all(upstream, "lev", split_axis=0, concat_axis=2, tiled=True)
    lon_sum = jnp.einsum("krj,jc->krc", full_rows, lon_table, preferred_element_type=jnp.float32)
    lon_coef = (lon_sum / NLON).astype(jnp.bfloat16)
    lat_table = wave_table(NLAT, MY, 0, NLAT)
    spectral = (
        jnp.einsum(
            "klc,ly->kcy",
            lax.all_to_all(lon_coef, "reg", split_axis=2, concat_axis=1, tiled=True),
            lat_table,
            preferred_element_type=jnp.float32,
        )
        / NLAT
    )
    share = spectral.shape[1]
    xindex = lax.axis_index("reg") * share + lax.iota(jnp.int32, share)
    level_count = spectral.shape[0] // FIELDS
    speeds = lax.dynamic_slice_in_dim(
        wave_speed, lax.axis_index("lev") * level_count, level_count, 0
    )
    solved = implicit_solve(spectral.reshape(level_count, FIELDS, share, 2 * MY), xindex, speeds)
    solved = solved.reshape(level_count * FIELDS, share, 2 * MY)
    back_lat = jnp.einsum(
        "kcy,ly->kcl", solved, lat_table, preferred_element_type=jnp.float32
    ).astype(jnp.bfloat16)
    back_coef = lax.all_to_all(back_lat, "reg", split_axis=2, concat_axis=1, tiled=True)
    own_table = wave_table(NLON, MX, col_first, cols_here)
    return jnp.einsum(
        "kcr,jc->krj",
        lax.all_gather(back_coef, "lev", axis=0, tiled=True),
        own_table,
        preferred_element_type=jnp.float32,
    ).astype(jnp.bfloat16)


def halo_parts(state):
    rows_here, cols_here = state.shape[1:]
    count = lax.axis_size("reg")
    forward = [(i, (i + 1) % count) for i in range(count)]
    backward = [(target, source) for source, target in forward]
    low = lax.ppermute(state[:, rows_here - HALO :], "reg", forward)
    high = lax.ppermute(state[:, :HALO], "reg", backward)
    edge = jnp.concatenate([low, high], axis=1)
    edge = jnp.pad(edge, ((0, 0), (0, ROWS - 2 * HALO), (0, 0)))
    tall = jnp.concatenate(
        [
            jnp.concatenate([part[:, :, :LANES], part[:, :, cols_here - LANES :]], axis=2)
            for part in (state, edge)
        ],
        axis=1,
    )
    lane = np.r_[0:HALO, 2 * LANES - HALO : 2 * LANES]
    pick = jnp.asarray((np.arange(2 * LANES)[:, None] == lane[None, :]), jnp.bfloat16)
    spot = np.r_[LANES : LANES + HALO, LANES - HALO : LANES]
    place = jnp.asarray((spot[:, None] == np.arange(2 * LANES)[None, :]), jnp.bfloat16)
    picked = jnp.einsum(
        "krl,le->ekr", tall, pick, preferred_element_type=jnp.float32
    ).astype(jnp.bfloat16)
    other = lax.ppermute(picked, "lev", [(0, 1), (1, 0)])
    pads = jnp.einsum(
        "ekr,el->krl", other, place, preferred_element_type=jnp.float32
    ).astype(jnp.bfloat16)
    levels = state.shape[0] // FIELDS
    return (
        edge.reshape(levels, FIELDS, ROWS, cols_here),
        pads.reshape(levels, FIELDS, rows_here + ROWS, 2 * LANES),
    )


def mux_pair(parts, bits):
    for bit, step in zip(bits, (4, 2, 1)):
        parts = [jnp.where(bit, parts[i + step], parts[i]) for i in range(len(parts) - step)]
    return parts


def interp_kernel(
    x_ref, edge_ref, pad_ref, dep_ref, weight_ref, out_ref, shift_ref, dep_t, weight_t, result_t
):
    levels, rows_here, cols_here = x_ref.shape
    chunk = out_ref.shape[2]
    taps = 2 * HALO + 1
    wide = chunk + 2 * LANES

    def shifted(block):
        block = jnp.swapaxes(block.astype(jnp.float32), 0, 1)
        flat = block.reshape(ROWS * levels, wide)
        for tap in range(taps):
            turned = pltpu.roll(flat, (HALO - tap) % wide, axis=1)[:, LANES : LANES + chunk]
            yield tap, turned.reshape(ROWS, levels, chunk)

    def spread(ref, rows, pad_rows, half):
        if half == 0:
            parts = [pad_ref[:, pad_rows, :LANES], ref[:, rows, : chunk + LANES]]
        else:
            parts = [ref[:, rows, chunk - LANES :], pad_ref[:, pad_rows, LANES:]]
        return jnp.concatenate(parts, axis=2)

    for half in range(2):

        @pl.when(pl.program_id(0) == half)
        def _():
            @pl.loop(0, rows_here // ROWS)
            def _(group):
                start = pl.multiple_of(group * ROWS, ROWS)
                rows = pl.ds(start, ROWS)
                for tap, turned in shifted(spread(x_ref, rows, rows, half)):
                    shift_ref[tap, pl.ds(start + HALO, ROWS)] = turned

            edge_rows = slice(rows_here, rows_here + ROWS)
            for tap, turned in shifted(spread(edge_ref, slice(0, ROWS), edge_rows, half)):
                shift_ref[tap, :HALO] = turned[:HALO]
                shift_ref[tap, rows_here + HALO :] = turned[HALO : 2 * HALO]

    pieces = chunk // LANES

    @pl.loop(0, rows_here // ROWS * pieces)
    def _(step):
        start = pl.multiple_of(step // pieces * ROWS, ROWS)
        cols = pl.ds(pl.multiple_of(step % pieces * LANES, LANES), LANES)
        dep_t[...] = jnp.swapaxes(dep_ref[:, pl.ds(start, ROWS), cols], 0, 1)
        weight_t[...] = jnp.swapaxes(weight_ref[:, pl.ds(start, ROWS), cols], 0, 1)

        @pl.loop(0, ROWS, step=2)
        def _(row0):
            for sub in range(2):
                row = row0 + sub
                cell = dep_t[row]
                row_bits = [(cell & bit) != 0 for bit in (32, 16, 8)]
                col_bits = [(cell & bit) != 0 for bit in (4, 2, 1)]
                low, high = [], []
                for tap in range(taps):
                    parts = [shift_ref[tap, start + row + i, :, cols] for i in range(taps)]
                    near, far = mux_pair(parts, row_bits)
                    low.append(near)
                    high.append(far)
                low = mux_pair(low, col_bits)
                high = mux_pair(high, col_bits)
                both = weight_t[row]
                high_part = (both * 241) >> 12
                weight_row = high_part.astype(jnp.float32) * (1.0 / 16.0)
                weight_col = (both - 17 * high_part).astype(jnp.float32) * (1.0 / 16.0)
                upper = (1.0 - weight_col) * low[0] + weight_col * low[1]
                lower = (1.0 - weight_col) * high[0] + weight_col * high[1]
                result_t[row] = (1.0 - weight_row) * upper + weight_row * lower

        done = jnp.swapaxes(result_t[...], 0, 1)
        out_ref[:, pl.ds(start, ROWS), cols] = done.astype(out_ref.dtype)


def interpolate(field, state, edge, pads, dep_cell, weight_code):
    levels, rows_here, cols_here = dep_cell.shape
    chunk = cols_here // 2
    taps = 2 * HALO + 1

    def of_field(array):
        return pl.BlockSpec((levels, None) + array.shape[2:], lambda h: (0, field, 0, 0))

    by_half = pl.BlockSpec((levels, rows_here, chunk), lambda h: (0, 0, h))
    return pl.pallas_call(
        interp_kernel,
        out_shape=jax.ShapeDtypeStruct((levels, rows_here, cols_here), jnp.bfloat16),
        grid=(2,),
        in_specs=[of_field(state), of_field(edge), of_field(pads), by_half, by_half],
        out_specs=by_half,
        scratch_shapes=[
            pltpu.VMEM((taps, rows_here + 2 * HALO, levels, chunk), jnp.float32),
            pltpu.VMEM((ROWS, levels, LANES), jnp.int32),
            pltpu.VMEM((ROWS, levels, LANES), jnp.int32),
            pltpu.VMEM((ROWS, levels, LANES), jnp.float32),
        ],
        compiler_params=pltpu.CompilerParams(vmem_limit_bytes=44 << 20),
        cost_estimate=pl.CostEstimate(
            flops=30 * 10**9, bytes_accessed=90 * 10**6, transcendentals=0
        ),
    )(state, edge, pads, dep_cell, weight_code)


def host_waves(length, wavenums, amount):
    angles = (np.arange(amount)[:, None] * wavenums[None, :] % length) * (2.0 * np.pi / length)
    both = np.stack([np.cos(angles), np.sin(angles)])
    return both.astype(np.float32).astype(ml_dtypes.bfloat16).transpose(0, 2, 1)


def solve_group(spectral, parity, speed):
    share = spectral[0].shape[0]
    wave_x = 2 * lax.iota(jnp.int32, share) + parity
    wave_y = lax.iota(jnp.int32, 2 * MY) % MY
    kx_term = 2.0 * math.pi / NLON * wave_x.astype(jnp.float32)
    ky_term = 2.0 * math.pi / NLAT * wave_y.astype(jnp.float32)
    laplace = kx_term[:, None] ** 2 + ky_term[None, :] ** 2
    inside = wave_x[:, None] * wave_x[:, None] + wave_y[None, :] * wave_y[None, :] < MX * MY
    weight_x = jnp.where(wave_x == 0, 1.0, 2.0)
    weight_y = jnp.where(wave_y == 0, 1.0, 2.0)
    factor = jnp.where(inside, weight_x[:, None] * weight_y[None, :], 0.0).astype(jnp.float32)
    div_new = (spectral[1] + laplace * spectral[2]) / (1.0 + speed * laplace)
    pres_new = spectral[2] - speed * div_new
    return [(part * factor).astype(jnp.bfloat16) for part in (spectral[0], div_new, pres_new)]


def synth_kernel(rows_ref, other_ref, own_ref, crossed_ref, *refs):
    out_ref = refs[-1]
    levels, rows_here, width = out_ref.shape
    total = 0.0
    for part_ref, table_ref in ((rows_ref, own_ref), (other_ref, crossed_ref)):
        for group in range(2):
            part = part_ref[group * levels : (group + 1) * levels]
            part = part.reshape(levels * rows_here, part.shape[2])
            total = total + jnp.dot(
                part, table_ref[group], preferred_element_type=jnp.float32
            )
    out_ref[...] = total.astype(out_ref.dtype).reshape(levels, rows_here, width)


def synthesize(field, rows, other, own, crossed, out):
    groups, rows_here, half = rows.shape
    levels = groups // 2
    cols_here = own.shape[2]
    block = 2 * LANES
    whole = pl.BlockSpec((groups, rows_here, half), lambda j: (0, 0, 0))
    table = pl.BlockSpec((2, half, block), lambda j: (0, 0, j))
    earlier = [] if out is None else [out]
    return pl.pallas_call(
        synth_kernel,
        out_shape=jax.ShapeDtypeStruct((levels, FIELDS, rows_here, cols_here), jnp.bfloat16),
        grid=(cols_here // block,),
        in_specs=[whole, whole, table, table] + [pl.BlockSpec(memory_space=pl.ANY)] * len(earlier),
        out_specs=pl.BlockSpec((levels, None, rows_here, block), lambda j: (0, field, 0, j)),
        input_output_aliases={4: 0} if earlier else {},
        compiler_params=pltpu.CompilerParams(vmem_limit_bytes=24 << 20),
        cost_estimate=pl.CostEstimate(
            flops=2 * 10**9, bytes_accessed=5 * 10**6, transcendentals=0
        ),
    )(rows, other, own, crossed, *earlier)


def paired_device(state_now, dep_cell, weight_code, wave_speed):
    stacked, rows_here, cols_here = state_now.shape
    levels = stacked // FIELDS
    swap = [(0, 1), (1, 0)]
    parity = lax.axis_index("lev")
    half = MX // 2
    even = jnp.asarray(host_waves(NLON, 2 * np.arange(half), cols_here))
    odd = jnp.asarray(host_waves(NLON, 2 * np.arange(half) + 1, cols_here))
    own = jnp.where(parity == 0, even, -odd)
    crossed = jnp.where(parity == 0, odd, even)
    lat = host_waves(NLAT, np.arange(MY), NLAT)
    lat = jnp.asarray(np.concatenate([lat[0], lat[1]], axis=0).T.copy())

    edge, pads = halo_parts(state_now)
    grouped = state_now.reshape(levels, FIELDS, rows_here, cols_here)
    spectral = []
    last = None
    for field in range(FIELDS):
        upstream = interpolate(field, grouped, edge, pads, dep_cell, weight_code)

        def partial_sum(table):
            return jnp.einsum(
                "vrj,gcj->gvrc", upstream, table, preferred_element_type=jnp.float32
            ) * (1.0 / NLON)

        leaving = partial_sum(crossed).astype(jnp.bfloat16)
        held = [leaving, edge] if last is None else [leaving, edge, last]
        leaving, edge = lax.optimization_barrier(held)[:2]
        away = lax.ppermute(leaving, "lev", swap)
        coef = (partial_sum(own) + away.astype(jnp.float32)).astype(jnp.bfloat16)
        last = coef
        coef = coef.reshape(2 * levels, rows_here, half)
        owned = lax.all_to_all(coef, "reg", split_axis=0, concat_axis=0, tiled=True)
        spectral.append(
            jnp.einsum(
                "lc,ly->cy", owned.reshape(NLAT, half), lat, preferred_element_type=jnp.float32
            )
            * (1.0 / NLAT)
        )
    speed = lax.dynamic_index_in_dim(wave_speed, lax.axis_index("reg") % levels, 0, keepdims=False)
    out = None
    for field, solved in enumerate(solve_group(spectral, parity, speed)):
        back = jnp.einsum(
            "ly,cy->lc", lat, solved, preferred_element_type=jnp.float32
        ).astype(jnp.bfloat16)
        back = back.reshape(2 * levels, rows_here, half)
        rows = lax.all_to_all(back, "reg", split_axis=0, concat_axis=0, tiled=True)
        other = lax.ppermute(rows, "lev", swap)
        out = synthesize(field, rows, other, own, crossed, out)
    return out.reshape(stacked, rows_here, cols_here)


def solution(mesh):
    placed = (P(None, "reg", "lev"), P(None, "reg", "lev"), P(None, "reg", "lev"), P())
    paired = mesh.shape["lev"] == 2 and mesh.shape["reg"] == 16
    return jax.shard_map(
        paired_device if paired else per_device,
        mesh=mesh,
        in_specs=placed,
        out_specs=P(None, "reg", "lev"),
        check_vma=False,
    )
```

```python
import math

import jax
import jax.numpy as jnp
import ml_dtypes
import numpy as np
from jax import lax
from jax.experimental import pallas as pl
from jax.experimental.pallas import tpu as pltpu
from jax.sharding import PartitionSpec as P

NLAT = 1280
NLON = 2560
MX = 640
MY = 640
FIELDS = 3
HALO = 4
LANES = 128
ROWS = 16


def padded_2(block, sides, width):
    for axis, dim in sides:
        count = lax.axis_size(axis)
        forward = [(i, i + 1) for i in range(count - 1)]
        forward.append((count - 1, 0))
        backward = [(target, source) for source, target in forward]
        low = lax.ppermute(
            lax.slice_in_dim(block, block.shape[dim] - width, None, axis=dim), axis, forward
        )
        high = lax.ppermute(lax.slice_in_dim(block, 0, width, axis=dim), axis, backward)
        block = jnp.concatenate([low, block, high], axis=dim)
    return block


def wave_table(length, modes, offset, amount):
    position = offset + lax.iota(jnp.int32, amount)
    wavenum = lax.iota(jnp.int32, 2 * modes) % modes
    product = position[:, None] * wavenum[None, :] % length
    angles = product.astype(jnp.float32) * (2.0 * math.pi / length)
    cosine_part = lax.iota(jnp.int32, 2 * modes) < modes
    return jnp.where(cosine_part[None, :], jnp.cos(angles), jnp.sin(angles)).astype(jnp.bfloat16)


def implicit_solve(spectral, xindex, speeds):
    wave_x = xindex % MX
    wave_y = lax.iota(jnp.int32, 2 * MY) % MY
    kx_term = 2.0 * math.pi / NLON * wave_x.astype(jnp.float32)
    ky_term = 2.0 * math.pi / NLAT * wave_y.astype(jnp.float32)
    laplace = kx_term[:, None] ** 2 + ky_term[None, :] ** 2
    inside = wave_x[:, None] * wave_x[:, None] + wave_y[None, :] * wave_y[None, :] < MX * MY
    weight_x = jnp.where(wave_x == 0, 1.0, 2.0)
    weight_y = jnp.where(wave_y == 0, 1.0, 2.0)
    factor = jnp.where(inside, weight_x[:, None] * weight_y[None, :], 0.0).astype(jnp.float32)
    speed_sq = speeds[:, None, None]
    vorticity = spectral[:, 0]
    divergence = spectral[:, 1]
    pressure = spectral[:, 2]
    div_new = (divergence + laplace * pressure) / (1.0 + speed_sq * laplace)
    pres_new = pressure - speed_sq * div_new
    stacked = jnp.stack([vorticity, div_new, pres_new], axis=1)
    return (stacked * factor[None, None]).astype(jnp.bfloat16)


def shift_weights(cell_code, code_index):
    shift_row = cell_code // (2 * HALO) - HALO
    shift_col = cell_code % (2 * HALO) - HALO
    weight_row = (code_index // 17).astype(jnp.float32) / 16.0
    weight_col = (code_index % 17).astype(jnp.float32) / 16.0
    row_weights = []
    col_weights = []
    for offset in range(-HALO, HALO + 1):
        row_weights.append(
            jnp.where(shift_row == offset, 1.0 - weight_row, 0.0)
            + jnp.where(shift_row + 1 == offset, weight_row, 0.0)
        )
        col_weights.append(
            jnp.where(shift_col == offset, 1.0 - weight_col, 0.0)
            + jnp.where(shift_col + 1 == offset, weight_col, 0.0)
        )
    return (row_weights, col_weights)


def interpolate_local(padded, row_weights, col_weights):
    levels, rows_pad, cols_pad = padded.shape
    rows_here = rows_pad - 2 * HALO
    cols_here = cols_pad - 2 * HALO
    blended = jnp.zeros((levels, rows_here, cols_here), jnp.float32)
    for row_step in range(2 * HALO + 1):
        inner = jnp.zeros((levels, rows_here, cols_here), jnp.float32)
        for col_step in range(2 * HALO + 1):
            window = padded[:, row_step : row_step + rows_here, col_step : col_step + cols_here]
            inner = inner + col_weights[col_step] * window.astype(jnp.float32)
        blended = blended + row_weights[row_step] * inner
    return blended.astype(jnp.bfloat16)


def per_device(state_now, dep_cell, weight_code, wave_speed):
    stacked, rows_here, cols_here = state_now.shape
    levels = stacked // FIELDS
    col_first = lax.axis_index("lev") * cols_here
    grouped = state_now.reshape(levels, FIELDS, rows_here, cols_here)
    row_weights, col_weights = shift_weights(dep_cell, weight_code)
    passes = []
    for which_field in range(FIELDS):
        padded = padded_2(grouped[:, which_field], (("reg", 1), ("lev", 2)), HALO)
        passes.append(interpolate_local(padded, row_weights, col_weights))
    upstream = jnp.stack(passes, axis=1).reshape(stacked, rows_here, cols_here)
    lon_table = wave_table(NLON, MX, 0, NLON)
    full_rows = lax.all_to_all(upstream, "lev", split_axis=0, concat_axis=2, tiled=True)
    lon_sum = jnp.einsum("krj,jc->krc", full_rows, lon_table, preferred_element_type=jnp.float32)
    lon_coef = (lon_sum / NLON).astype(jnp.bfloat16)
    lat_table = wave_table(NLAT, MY, 0, NLAT)
    spectral = (
        jnp.einsum(
            "klc,ly->kcy",
            lax.all_to_all(lon_coef, "reg", split_axis=2, concat_axis=1, tiled=True),
            lat_table,
            preferred_element_type=jnp.float32,
        )
        / NLAT
    )
    share = spectral.shape[1]
    xindex = lax.axis_index("reg") * share + lax.iota(jnp.int32, share)
    level_count = spectral.shape[0] // FIELDS
    speeds = lax.dynamic_slice_in_dim(
        wave_speed, lax.axis_index("lev") * level_count, level_count, 0
    )
    solved = implicit_solve(spectral.reshape(level_count, FIELDS, share, 2 * MY), xindex, speeds)
    solved = solved.reshape(level_count * FIELDS, share, 2 * MY)
    back_lat = jnp.einsum(
        "kcy,ly->kcl", solved, lat_table, preferred_element_type=jnp.float32
    ).astype(jnp.bfloat16)
    back_coef = lax.all_to_all(back_lat, "reg", split_axis=2, concat_axis=1, tiled=True)
    own_table = wave_table(NLON, MX, col_first, cols_here)
    return jnp.einsum(
        "kcr,jc->krj",
        lax.all_gather(back_coef, "lev", axis=0, tiled=True),
        own_table,
        preferred_element_type=jnp.float32,
    ).astype(jnp.bfloat16)


def halo_parts(state):
    rows_here, cols_here = state.shape[1:]
    count = lax.axis_size("reg")
    forward = [(i, (i + 1) % count) for i in range(count)]
    backward = [(target, source) for source, target in forward]
    low = lax.ppermute(state[:, rows_here - HALO :], "reg", forward)
    high = lax.ppermute(state[:, :HALO], "reg", backward)
    edge = jnp.concatenate([low, high], axis=1)
    edge = jnp.pad(edge, ((0, 0), (0, ROWS - 2 * HALO), (0, 0)))
    tall = jnp.concatenate(
        [
            jnp.concatenate([part[:, :, :LANES], part[:, :, cols_here - LANES :]], axis=2)
            for part in (state, edge)
        ],
        axis=1,
    )
    lane = np.r_[0:HALO, 2 * LANES - HALO : 2 * LANES]
    pick = jnp.asarray((np.arange(2 * LANES)[:, None] == lane[None, :]), jnp.bfloat16)
    spot = np.r_[LANES : LANES + HALO, LANES - HALO : LANES]
    place = jnp.asarray((spot[:, None] == np.arange(2 * LANES)[None, :]), jnp.bfloat16)
    picked = jnp.einsum(
        "krl,le->ekr", tall, pick, preferred_element_type=jnp.float32
    ).astype(jnp.bfloat16)
    other = lax.ppermute(picked, "lev", [(0, 1), (1, 0)])
    pads = jnp.einsum(
        "ekr,el->krl", other, place, preferred_element_type=jnp.float32
    ).astype(jnp.bfloat16)
    levels = state.shape[0] // FIELDS
    return (
        edge.reshape(levels, FIELDS, ROWS, cols_here),
        pads.reshape(levels, FIELDS, rows_here + ROWS, 2 * LANES),
    )


def mux_pair(parts, bits):
    for bit, step in zip(bits, (4, 2, 1)):
        parts = [jnp.where(bit, parts[i + step], parts[i]) for i in range(len(parts) - step)]
    return parts


def interp_kernel(
    x_ref, edge_ref, pad_ref, dep_ref, weight_ref, out_ref, shift_ref, dep_t, weight_t, result_t
):
    levels, rows_here, cols_here = x_ref.shape
    chunk = cols_here // 2
    lanes = 2 * levels
    taps = 2 * HALO + 1
    wide = chunk + 2 * LANES

    def shifted(ref, rows, pad_rows):
        left = jnp.concatenate(
            [pad_ref[:, pad_rows, :LANES], ref[:, rows, : chunk + LANES]], axis=2
        )
        right = jnp.concatenate(
            [ref[:, rows, chunk - LANES :], pad_ref[:, pad_rows, LANES:]], axis=2
        )
        block = jnp.concatenate([left, right], axis=0).astype(jnp.float32)
        block = jnp.swapaxes(block, 0, 1)
        flat = block.reshape(ROWS * lanes, wide)
        for tap in range(taps):
            turned = pltpu.roll(flat, (HALO - tap) % wide, axis=1)[:, LANES : LANES + chunk]
            yield tap, turned.astype(jnp.bfloat16).reshape(ROWS, lanes, chunk)

    @pl.loop(0, rows_here // ROWS)
    def _(group):
        start = pl.multiple_of(group * ROWS, ROWS)
        rows = pl.ds(start, ROWS)
        for tap, turned in shifted(x_ref, rows, rows):
            shift_ref[tap, pl.ds(start + HALO, ROWS)] = turned

    edge_rows = slice(rows_here, rows_here + ROWS)
    for tap, turned in shifted(edge_ref, slice(0, ROWS), edge_rows):
        shift_ref[tap, :HALO] = turned[:HALO]
        shift_ref[tap, rows_here + HALO :] = turned[HALO : 2 * HALO]

    pieces = chunk // LANES

    def both_halves(ref, rows, col):
        parts = [ref[:, rows, pl.ds(pl.multiple_of(col + h * chunk, LANES), LANES)] for h in range(2)]
        return jnp.swapaxes(jnp.concatenate(parts, axis=0), 0, 1)

    @pl.loop(0, rows_here // ROWS * pieces)
    def _(step):
        start = pl.multiple_of(step // pieces * ROWS, ROWS)
        col = pl.multiple_of(step % pieces * LANES, LANES)
        cols = pl.ds(col, LANES)
        dep_t[...] = both_halves(dep_ref, pl.ds(start, ROWS), col)
        weight_t[...] = both_halves(weight_ref, pl.ds(start, ROWS), col)

        @pl.loop(0, ROWS, step=2)
        def _(row0):
            for sub in range(2):
                row = row0 + sub
                cell = dep_t[row]
                masks = [
                    (cell & bit).astype(jnp.float32).astype(jnp.bfloat16) > 0
                    for bit in (32, 16, 8, 4, 2, 1)
                ]
                low, high = [], []
                for tap in range(taps):
                    parts = [shift_ref[tap, start + row + i, :, cols] for i in range(taps)]
                    near, far = mux_pair(parts, masks[:3])
                    low.append(near)
                    high.append(far)
                low = [part.astype(jnp.float32) for part in mux_pair(low, masks[3:])]
                high = [part.astype(jnp.float32) for part in mux_pair(high, masks[3:])]
                both = weight_t[row]
                high_part = (both * 241) >> 12
                weight_row = high_part.astype(jnp.float32) * (1.0 / 16.0)
                weight_col = (both - 17 * high_part).astype(jnp.float32) * (1.0 / 16.0)
                upper = (1.0 - weight_col) * low[0] + weight_col * low[1]
                lower = (1.0 - weight_col) * high[0] + weight_col * high[1]
                result_t[row] = (1.0 - weight_row) * upper + weight_row * lower

        done = jnp.swapaxes(result_t[...], 0, 1).astype(out_ref.dtype)
        for h in range(2):
            place = pl.ds(pl.multiple_of(col + h * chunk, LANES), LANES)
            out_ref[:, pl.ds(start, ROWS), place] = done[h * levels : (h + 1) * levels]


def interpolate(field, state, edge, pads, dep_cell, weight_code):
    levels, rows_here, cols_here = dep_cell.shape
    taps = 2 * HALO + 1

    def of_field(array):
        return pl.BlockSpec((levels, None) + array.shape[2:], lambda h: (0, field, 0, 0))

    whole = pl.BlockSpec((levels, rows_here, cols_here), lambda h: (0, 0, 0))
    return pl.pallas_call(
        interp_kernel,
        out_shape=jax.ShapeDtypeStruct((levels, rows_here, cols_here), jnp.bfloat16),
        grid=(1,),
        in_specs=[of_field(state), of_field(edge), of_field(pads), whole, whole],
        out_specs=whole,
        scratch_shapes=[
            pltpu.VMEM((taps, rows_here + 2 * HALO, 2 * levels, cols_here // 2), jnp.bfloat16),
            pltpu.VMEM((ROWS, 2 * levels, LANES), jnp.int32),
            pltpu.VMEM((ROWS, 2 * levels, LANES), jnp.int32),
            pltpu.VMEM((ROWS, 2 * levels, LANES), jnp.float32),
        ],
        compiler_params=pltpu.CompilerParams(vmem_limit_bytes=44 << 20),
        cost_estimate=pl.CostEstimate(
            flops=30 * 10**9, bytes_accessed=90 * 10**6, transcendentals=0
        ),
    )(state, edge, pads, dep_cell, weight_code)


def host_waves(length, wavenums, amount):
    angles = (np.arange(amount)[:, None] * wavenums[None, :] % length) * (2.0 * np.pi / length)
    both = np.stack([np.cos(angles), np.sin(angles)])
    return both.astype(np.float32).astype(ml_dtypes.bfloat16).transpose(0, 2, 1)


def solve_group(spectral, parity, speed):
    share = spectral[0].shape[0]
    wave_x = 2 * lax.iota(jnp.int32, share) + parity
    wave_y = lax.iota(jnp.int32, 2 * MY) % MY
    kx_term = 2.0 * math.pi / NLON * wave_x.astype(jnp.float32)
    ky_term = 2.0 * math.pi / NLAT * wave_y.astype(jnp.float32)
    laplace = kx_term[:, None] ** 2 + ky_term[None, :] ** 2
    inside = wave_x[:, None] * wave_x[:, None] + wave_y[None, :] * wave_y[None, :] < MX * MY
    weight_x = jnp.where(wave_x == 0, 1.0, 2.0)
    weight_y = jnp.where(wave_y == 0, 1.0, 2.0)
    factor = jnp.where(inside, weight_x[:, None] * weight_y[None, :], 0.0).astype(jnp.float32)
    div_new = (spectral[1] + laplace * spectral[2]) / (1.0 + speed * laplace)
    pres_new = spectral[2] - speed * div_new
    return [(part * factor).astype(jnp.bfloat16) for part in (spectral[0], div_new, pres_new)]


def synth_kernel(rows_ref, other_ref, own_ref, crossed_ref, *refs):
    out_ref = refs[-1]
    levels, rows_here, width = out_ref.shape
    total = 0.0
    for part_ref, table_ref in ((rows_ref, own_ref), (other_ref, crossed_ref)):
        for group in range(2):
            part = part_ref[group * levels : (group + 1) * levels]
            part = part.reshape(levels * rows_here, part.shape[2])
            total = total + jnp.dot(
                part, table_ref[group], preferred_element_type=jnp.float32
            )
    out_ref[...] = total.astype(out_ref.dtype).reshape(levels, rows_here, width)


def synthesize(field, rows, other, own, crossed, out):
    groups, rows_here, half = rows.shape
    levels = groups // 2
    cols_here = own.shape[2]
    block = 2 * LANES
    whole = pl.BlockSpec((groups, rows_here, half), lambda j: (0, 0, 0))
    table = pl.BlockSpec((2, half, block), lambda j: (0, 0, j))
    earlier = [] if out is None else [out]
    return pl.pallas_call(
        synth_kernel,
        out_shape=jax.ShapeDtypeStruct((levels, FIELDS, rows_here, cols_here), jnp.bfloat16),
        grid=(cols_here // block,),
        in_specs=[whole, whole, table, table] + [pl.BlockSpec(memory_space=pl.ANY)] * len(earlier),
        out_specs=pl.BlockSpec((levels, None, rows_here, block), lambda j: (0, field, 0, j)),
        input_output_aliases={4: 0} if earlier else {},
        compiler_params=pltpu.CompilerParams(vmem_limit_bytes=24 << 20),
        cost_estimate=pl.CostEstimate(
            flops=2 * 10**9, bytes_accessed=5 * 10**6, transcendentals=0
        ),
    )(rows, other, own, crossed, *earlier)


def paired_device(state_now, dep_cell, weight_code, wave_speed):
    stacked, rows_here, cols_here = state_now.shape
    levels = stacked // FIELDS
    swap = [(0, 1), (1, 0)]
    parity = lax.axis_index("lev")
    half = MX // 2
    even = jnp.asarray(host_waves(NLON, 2 * np.arange(half), cols_here))
    odd = jnp.asarray(host_waves(NLON, 2 * np.arange(half) + 1, cols_here))
    own = jnp.where(parity == 0, even, -odd)
    crossed = jnp.where(parity == 0, odd, even)
    lat = host_waves(NLAT, np.arange(MY), NLAT)
    lat = jnp.asarray(np.concatenate([lat[0], lat[1]], axis=0).T.copy())

    edge, pads = halo_parts(state_now)
    grouped = state_now.reshape(levels, FIELDS, rows_here, cols_here)
    spectral = []
    last = None
    for field in range(FIELDS):
        upstream = interpolate(field, grouped, edge, pads, dep_cell, weight_code)

        def partial_sum(table):
            return jnp.einsum(
                "vrj,gcj->gvrc", upstream, table, preferred_element_type=jnp.float32
            ) * (1.0 / NLON)

        leaving = partial_sum(crossed).astype(jnp.bfloat16)
        held = [leaving, edge] if last is None else [leaving, edge, last]
        leaving, edge = lax.optimization_barrier(held)[:2]
        away = lax.ppermute(leaving, "lev", swap)
        coef = (partial_sum(own) + away.astype(jnp.float32)).astype(jnp.bfloat16)
        last = coef
        coef = coef.reshape(2 * levels, rows_here, half)
        owned = lax.all_to_all(coef, "reg", split_axis=0, concat_axis=0, tiled=True)
        spectral.append(
            jnp.einsum(
                "lc,ly->cy", owned.reshape(NLAT, half), lat, preferred_element_type=jnp.float32
            )
            * (1.0 / NLAT)
        )
    speed = lax.dynamic_index_in_dim(wave_speed, lax.axis_index("reg") % levels, 0, keepdims=False)
    out, others = None, []
    for field, solved in enumerate(solve_group(spectral, parity, speed)):
        back = jnp.einsum(
            "ly,cy->lc", lat, solved, preferred_element_type=jnp.float32
        ).astype(jnp.bfloat16)
        back = back.reshape(2 * levels, rows_here, half)
        if field == 2:
            back = lax.optimization_barrier((back, others[0]))[0]
        rows = lax.all_to_all(back, "reg", split_axis=0, concat_axis=0, tiled=True)
        if field == 2:
            rows = lax.optimization_barrier((rows, others[1]))[0]
        other = lax.ppermute(rows, "lev", swap)
        others.append(other)
        out = synthesize(field, rows, other, own, crossed, out)
    return out.reshape(stacked, rows_here, cols_here)


def solution(mesh):
    placed = (P(None, "reg", "lev"), P(None, "reg", "lev"), P(None, "reg", "lev"), P())
    paired = mesh.shape["lev"] == 2 and mesh.shape["reg"] == 16
    return jax.shard_map(
        paired_device if paired else per_device,
        mesh=mesh,
        in_specs=placed,
        out_specs=P(None, "reg", "lev"),
        check_vma=False,
    )
```

```python
import math

import jax
import jax.numpy as jnp
import ml_dtypes
import numpy as np
from jax import lax
from jax.experimental import pallas as pl
from jax.experimental.pallas import tpu as pltpu
from jax.sharding import PartitionSpec as P

NLAT = 1280
NLON = 2560
MX = 640
MY = 640
FIELDS = 3
HALO = 4
LANES = 128
ROWS = 16


def padded_2(block, sides, width):
    for axis, dim in sides:
        count = lax.axis_size(axis)
        forward = [(i, i + 1) for i in range(count - 1)]
        forward.append((count - 1, 0))
        backward = [(target, source) for source, target in forward]
        low = lax.ppermute(
            lax.slice_in_dim(block, block.shape[dim] - width, None, axis=dim), axis, forward
        )
        high = lax.ppermute(lax.slice_in_dim(block, 0, width, axis=dim), axis, backward)
        block = jnp.concatenate([low, block, high], axis=dim)
    return block


def wave_table(length, modes, offset, amount):
    position = offset + lax.iota(jnp.int32, amount)
    wavenum = lax.iota(jnp.int32, 2 * modes) % modes
    product = position[:, None] * wavenum[None, :] % length
    angles = product.astype(jnp.float32) * (2.0 * math.pi / length)
    cosine_part = lax.iota(jnp.int32, 2 * modes) < modes
    return jnp.where(cosine_part[None, :], jnp.cos(angles), jnp.sin(angles)).astype(jnp.bfloat16)


def implicit_solve(spectral, xindex, speeds):
    wave_x = xindex % MX
    wave_y = lax.iota(jnp.int32, 2 * MY) % MY
    kx_term = 2.0 * math.pi / NLON * wave_x.astype(jnp.float32)
    ky_term = 2.0 * math.pi / NLAT * wave_y.astype(jnp.float32)
    laplace = kx_term[:, None] ** 2 + ky_term[None, :] ** 2
    inside = wave_x[:, None] * wave_x[:, None] + wave_y[None, :] * wave_y[None, :] < MX * MY
    weight_x = jnp.where(wave_x == 0, 1.0, 2.0)
    weight_y = jnp.where(wave_y == 0, 1.0, 2.0)
    factor = jnp.where(inside, weight_x[:, None] * weight_y[None, :], 0.0).astype(jnp.float32)
    speed_sq = speeds[:, None, None]
    vorticity = spectral[:, 0]
    divergence = spectral[:, 1]
    pressure = spectral[:, 2]
    div_new = (divergence + laplace * pressure) / (1.0 + speed_sq * laplace)
    pres_new = pressure - speed_sq * div_new
    stacked = jnp.stack([vorticity, div_new, pres_new], axis=1)
    return (stacked * factor[None, None]).astype(jnp.bfloat16)


def shift_weights(cell_code, code_index):
    shift_row = cell_code // (2 * HALO) - HALO
    shift_col = cell_code % (2 * HALO) - HALO
    weight_row = (code_index // 17).astype(jnp.float32) / 16.0
    weight_col = (code_index % 17).astype(jnp.float32) / 16.0
    row_weights = []
    col_weights = []
    for offset in range(-HALO, HALO + 1):
        row_weights.append(
            jnp.where(shift_row == offset, 1.0 - weight_row, 0.0)
            + jnp.where(shift_row + 1 == offset, weight_row, 0.0)
        )
        col_weights.append(
            jnp.where(shift_col == offset, 1.0 - weight_col, 0.0)
            + jnp.where(shift_col + 1 == offset, weight_col, 0.0)
        )
    return (row_weights, col_weights)


def interpolate_local(padded, row_weights, col_weights):
    levels, rows_pad, cols_pad = padded.shape
    rows_here = rows_pad - 2 * HALO
    cols_here = cols_pad - 2 * HALO
    blended = jnp.zeros((levels, rows_here, cols_here), jnp.float32)
    for row_step in range(2 * HALO + 1):
        inner = jnp.zeros((levels, rows_here, cols_here), jnp.float32)
        for col_step in range(2 * HALO + 1):
            window = padded[:, row_step : row_step + rows_here, col_step : col_step + cols_here]
            inner = inner + col_weights[col_step] * window.astype(jnp.float32)
        blended = blended + row_weights[row_step] * inner
    return blended.astype(jnp.bfloat16)


def per_device(state_now, dep_cell, weight_code, wave_speed):
    stacked, rows_here, cols_here = state_now.shape
    levels = stacked // FIELDS
    col_first = lax.axis_index("lev") * cols_here
    grouped = state_now.reshape(levels, FIELDS, rows_here, cols_here)
    row_weights, col_weights = shift_weights(dep_cell, weight_code)
    passes = []
    for which_field in range(FIELDS):
        padded = padded_2(grouped[:, which_field], (("reg", 1), ("lev", 2)), HALO)
        passes.append(interpolate_local(padded, row_weights, col_weights))
    upstream = jnp.stack(passes, axis=1).reshape(stacked, rows_here, cols_here)
    lon_table = wave_table(NLON, MX, 0, NLON)
    full_rows = lax.all_to_all(upstream, "lev", split_axis=0, concat_axis=2, tiled=True)
    lon_sum = jnp.einsum("krj,jc->krc", full_rows, lon_table, preferred_element_type=jnp.float32)
    lon_coef = (lon_sum / NLON).astype(jnp.bfloat16)
    lat_table = wave_table(NLAT, MY, 0, NLAT)
    spectral = (
        jnp.einsum(
            "klc,ly->kcy",
            lax.all_to_all(lon_coef, "reg", split_axis=2, concat_axis=1, tiled=True),
            lat_table,
            preferred_element_type=jnp.float32,
        )
        / NLAT
    )
    share = spectral.shape[1]
    xindex = lax.axis_index("reg") * share + lax.iota(jnp.int32, share)
    level_count = spectral.shape[0] // FIELDS
    speeds = lax.dynamic_slice_in_dim(
        wave_speed, lax.axis_index("lev") * level_count, level_count, 0
    )
    solved = implicit_solve(spectral.reshape(level_count, FIELDS, share, 2 * MY), xindex, speeds)
    solved = solved.reshape(level_count * FIELDS, share, 2 * MY)
    back_lat = jnp.einsum(
        "kcy,ly->kcl", solved, lat_table, preferred_element_type=jnp.float32
    ).astype(jnp.bfloat16)
    back_coef = lax.all_to_all(back_lat, "reg", split_axis=2, concat_axis=1, tiled=True)
    own_table = wave_table(NLON, MX, col_first, cols_here)
    return jnp.einsum(
        "kcr,jc->krj",
        lax.all_gather(back_coef, "lev", axis=0, tiled=True),
        own_table,
        preferred_element_type=jnp.float32,
    ).astype(jnp.bfloat16)


def halo_parts(state):
    rows_here, cols_here = state.shape[1:]
    count = lax.axis_size("reg")
    forward = [(i, (i + 1) % count) for i in range(count)]
    backward = [(target, source) for source, target in forward]
    low = lax.ppermute(state[:, rows_here - HALO :], "reg", forward)
    high = lax.ppermute(state[:, :HALO], "reg", backward)
    edge = jnp.concatenate([low, high], axis=1)
    edge = jnp.pad(edge, ((0, 0), (0, ROWS - 2 * HALO), (0, 0)))
    tall = jnp.concatenate(
        [
            jnp.concatenate([part[:, :, :LANES], part[:, :, cols_here - LANES :]], axis=2)
            for part in (state, edge)
        ],
        axis=1,
    )
    lane = np.r_[0:HALO, 2 * LANES - HALO : 2 * LANES]
    pick = jnp.asarray((np.arange(2 * LANES)[:, None] == lane[None, :]), jnp.bfloat16)
    spot = np.r_[LANES : LANES + HALO, LANES - HALO : LANES]
    place = jnp.asarray((spot[:, None] == np.arange(2 * LANES)[None, :]), jnp.bfloat16)
    picked = jnp.einsum(
        "krl,le->ekr", tall, pick, preferred_element_type=jnp.float32
    ).astype(jnp.bfloat16)
    other = lax.ppermute(picked, "lev", [(0, 1), (1, 0)])
    pads = jnp.einsum(
        "ekr,el->krl", other, place, preferred_element_type=jnp.float32
    ).astype(jnp.bfloat16)
    levels = state.shape[0] // FIELDS
    return (
        edge.reshape(levels, FIELDS, ROWS, cols_here),
        pads.reshape(levels, FIELDS, rows_here + ROWS, 2 * LANES),
    )


def mux_pair(parts, bits):
    for bit, step in zip(bits, (4, 2, 1)):
        parts = [jnp.where(bit, parts[i + step], parts[i]) for i in range(len(parts) - step)]
    return parts


def interp_kernel(
    x_ref, edge_ref, pad_ref, dep_ref, weight_ref, out_ref, shift_ref, dep_t, weight_t, result_t
):
    levels, rows_here, cols_here = x_ref.shape
    chunk = cols_here // 2
    lanes = 2 * levels
    taps = 2 * HALO + 1
    wide = chunk + 2 * LANES

    def shifted(ref, rows, pad_rows):
        left = jnp.concatenate(
            [pad_ref[:, pad_rows, :LANES], ref[:, rows, : chunk + LANES]], axis=2
        )
        right = jnp.concatenate(
            [ref[:, rows, chunk - LANES :], pad_ref[:, pad_rows, LANES:]], axis=2
        )
        block = jnp.concatenate([left, right], axis=0).astype(jnp.float32)
        block = jnp.swapaxes(block, 0, 1)
        flat = block.reshape(ROWS * lanes, wide)
        for tap in range(taps):
            turned = pltpu.roll(flat, (HALO - tap) % wide, axis=1)[:, LANES : LANES + chunk]
            yield tap, turned.astype(jnp.bfloat16).reshape(ROWS, lanes, chunk)

    @pl.loop(0, rows_here // ROWS)
    def _(group):
        start = pl.multiple_of(group * ROWS, ROWS)
        rows = pl.ds(start, ROWS)
        for tap, turned in shifted(x_ref, rows, rows):
            shift_ref[tap, pl.ds(start + HALO, ROWS)] = turned

    edge_rows = slice(rows_here, rows_here + ROWS)
    for tap, turned in shifted(edge_ref, slice(0, ROWS), edge_rows):
        shift_ref[tap, :HALO] = turned[:HALO]
        shift_ref[tap, rows_here + HALO :] = turned[HALO : 2 * HALO]

    pieces = chunk // LANES

    def both_halves(ref, rows, col):
        parts = [ref[:, rows, pl.ds(pl.multiple_of(col + h * chunk, LANES), LANES)] for h in range(2)]
        return jnp.swapaxes(jnp.concatenate(parts, axis=0), 0, 1)

    @pl.loop(0, rows_here // ROWS * pieces)
    def _(step):
        start = pl.multiple_of(step // pieces * ROWS, ROWS)
        col = pl.multiple_of(step % pieces * LANES, LANES)
        cols = pl.ds(col, LANES)
        dep_t[...] = both_halves(dep_ref, pl.ds(start, ROWS), col)
        weight_t[...] = both_halves(weight_ref, pl.ds(start, ROWS), col)

        @pl.loop(0, ROWS, step=2)
        def _(row0):
            for sub in range(2):
                row = row0 + sub
                cell = dep_t[row]
                masks = [
                    (cell & bit).astype(jnp.float32).astype(jnp.bfloat16) > 0
                    for bit in (32, 16, 8, 4, 2, 1)
                ]
                low, high = [], []
                for tap in range(taps):
                    parts = [shift_ref[tap, start + row + i, :, cols] for i in range(taps)]
                    near, far = mux_pair(parts, masks[:3])
                    low.append(near)
                    high.append(far)
                low = [part.astype(jnp.float32) for part in mux_pair(low, masks[3:])]
                high = [part.astype(jnp.float32) for part in mux_pair(high, masks[3:])]
                both = weight_t[row]
                high_part = (both * 241) >> 12
                weight_row = high_part.astype(jnp.float32) * (1.0 / 16.0)
                weight_col = (both - 17 * high_part).astype(jnp.float32) * (1.0 / 16.0)
                upper = (1.0 - weight_col) * low[0] + weight_col * low[1]
                lower = (1.0 - weight_col) * high[0] + weight_col * high[1]
                result_t[row] = (1.0 - weight_row) * upper + weight_row * lower

        done = jnp.swapaxes(result_t[...], 0, 1).astype(out_ref.dtype)
        for h in range(2):
            place = pl.ds(pl.multiple_of(col + h * chunk, LANES), LANES)
            out_ref[:, pl.ds(start, ROWS), place] = done[h * levels : (h + 1) * levels]


def interpolate(field, state, edge, pads, dep_cell, weight_code):
    levels, rows_here, cols_here = dep_cell.shape
    taps = 2 * HALO + 1

    def of_field(array):
        return pl.BlockSpec((levels, None) + array.shape[2:], lambda h: (0, field, 0, 0))

    whole = pl.BlockSpec((levels, rows_here, cols_here), lambda h: (0, 0, 0))
    return pl.pallas_call(
        interp_kernel,
        out_shape=jax.ShapeDtypeStruct((levels, rows_here, cols_here), jnp.bfloat16),
        grid=(1,),
        in_specs=[of_field(state), of_field(edge), of_field(pads), whole, whole],
        out_specs=whole,
        scratch_shapes=[
            pltpu.VMEM((taps, rows_here + 2 * HALO, 2 * levels, cols_here // 2), jnp.bfloat16),
            pltpu.VMEM((ROWS, 2 * levels, LANES), jnp.int32),
            pltpu.VMEM((ROWS, 2 * levels, LANES), jnp.int32),
            pltpu.VMEM((ROWS, 2 * levels, LANES), jnp.float32),
        ],
        compiler_params=pltpu.CompilerParams(vmem_limit_bytes=44 << 20),
        cost_estimate=pl.CostEstimate(
            flops=30 * 10**9, bytes_accessed=90 * 10**6, transcendentals=0
        ),
    )(state, edge, pads, dep_cell, weight_code)


def host_waves(length, wavenums, amount):
    angles = (np.arange(amount)[:, None] * wavenums[None, :] % length) * (2.0 * np.pi / length)
    both = np.stack([np.cos(angles), np.sin(angles)])
    return both.astype(np.float32).astype(ml_dtypes.bfloat16).transpose(0, 2, 1)


def solve_group(spectral, parity, speed):
    share = spectral[0].shape[0]
    wave_x = 2 * lax.iota(jnp.int32, share) + parity
    wave_y = lax.iota(jnp.int32, 2 * MY) % MY
    kx_term = 2.0 * math.pi / NLON * wave_x.astype(jnp.float32)
    ky_term = 2.0 * math.pi / NLAT * wave_y.astype(jnp.float32)
    laplace = kx_term[:, None] ** 2 + ky_term[None, :] ** 2
    inside = wave_x[:, None] * wave_x[:, None] + wave_y[None, :] * wave_y[None, :] < MX * MY
    weight_x = jnp.where(wave_x == 0, 1.0, 2.0)
    weight_y = jnp.where(wave_y == 0, 1.0, 2.0)
    factor = jnp.where(inside, weight_x[:, None] * weight_y[None, :], 0.0).astype(jnp.float32)
    div_new = (spectral[1] + laplace * spectral[2]) / (1.0 + speed * laplace)
    pres_new = spectral[2] - speed * div_new
    return [(part * factor).astype(jnp.bfloat16) for part in (spectral[0], div_new, pres_new)]


def synth_kernel(rows_ref, other_ref, own_ref, crossed_ref, *refs):
    out_ref = refs[-1]
    levels, rows_here, width = out_ref.shape
    total = 0.0
    for part_ref, table_ref in ((rows_ref, own_ref), (other_ref, crossed_ref)):
        for group in range(2):
            part = part_ref[group * levels : (group + 1) * levels]
            part = part.reshape(levels * rows_here, part.shape[2])
            total = total + jnp.dot(
                part, table_ref[group], preferred_element_type=jnp.float32
            )
    out_ref[...] = total.astype(out_ref.dtype).reshape(levels, rows_here, width)


def synthesize(field, rows, other, own, crossed, out):
    groups, rows_here, half = rows.shape
    levels = groups // 2
    cols_here = own.shape[2]
    block = 2 * LANES
    whole = pl.BlockSpec((groups, rows_here, half), lambda j: (0, 0, 0))
    table = pl.BlockSpec((2, half, block), lambda j: (0, 0, j))
    earlier = [] if out is None else [out]
    return pl.pallas_call(
        synth_kernel,
        out_shape=jax.ShapeDtypeStruct((levels, FIELDS, rows_here, cols_here), jnp.bfloat16),
        grid=(cols_here // block,),
        in_specs=[whole, whole, table, table] + [pl.BlockSpec(memory_space=pl.ANY)] * len(earlier),
        out_specs=pl.BlockSpec((levels, None, rows_here, block), lambda j: (0, field, 0, j)),
        input_output_aliases={4: 0} if earlier else {},
        compiler_params=pltpu.CompilerParams(vmem_limit_bytes=24 << 20),
        cost_estimate=pl.CostEstimate(
            flops=2 * 10**9, bytes_accessed=5 * 10**6, transcendentals=0
        ),
    )(rows, other, own, crossed, *earlier)


def paired_device(state_now, dep_cell, weight_code, wave_speed):
    stacked, rows_here, cols_here = state_now.shape
    levels = stacked // FIELDS
    swap = [(0, 1), (1, 0)]
    parity = lax.axis_index("lev")
    half = MX // 2
    even = jnp.asarray(host_waves(NLON, 2 * np.arange(half), cols_here))
    odd = jnp.asarray(host_waves(NLON, 2 * np.arange(half) + 1, cols_here))
    own = jnp.where(parity == 0, even, -odd)
    crossed = jnp.where(parity == 0, odd, even)
    lat = host_waves(NLAT, np.arange(MY), NLAT)
    lat = jnp.asarray(np.concatenate([lat[0], lat[1]], axis=0).T.copy())

    edge, pads = halo_parts(state_now)
    grouped = state_now.reshape(levels, FIELDS, rows_here, cols_here)
    def partial_sum(upstream, table):
        return jnp.einsum(
            "vrj,gcj->gvrc", upstream, table, preferred_element_type=jnp.float32
        ) * (1.0 / NLON)

    def whole_sum(upstream, away):
        total = partial_sum(upstream, own) + away.astype(jnp.float32)
        return total.astype(jnp.bfloat16)

    def to_spectral(coef):
        coef = coef.reshape(2 * levels, rows_here, half)
        owned = lax.all_to_all(coef, "reg", split_axis=0, concat_axis=0, tiled=True)
        return jnp.einsum(
            "lc,ly->cy", owned.reshape(NLAT, half), lat, preferred_element_type=jnp.float32
        ) * (1.0 / NLAT)

    spectral = []
    before = None
    for field in range(FIELDS):
        upstream = interpolate(field, grouped, edge, pads, dep_cell, weight_code)
        leaving = partial_sum(upstream, crossed).astype(jnp.bfloat16)
        if before is None:
            leaving, edge = lax.optimization_barrier((leaving, edge))
        else:
            leaving, away = lax.optimization_barrier((leaving, before[1]))
            coef = whole_sum(before[0], away)
            coef, edge, _ = lax.optimization_barrier((coef, edge, leaving))
            spectral.append(to_spectral(coef))
        before = (upstream, lax.ppermute(leaving, "lev", swap))
    spectral.append(to_spectral(whole_sum(*before)))
    speed = lax.dynamic_index_in_dim(wave_speed, lax.axis_index("reg") % levels, 0, keepdims=False)
    out, others = None, []
    for field, solved in enumerate(solve_group(spectral, parity, speed)):
        back = jnp.einsum(
            "ly,cy->lc", lat, solved, preferred_element_type=jnp.float32
        ).astype(jnp.bfloat16)
        back = back.reshape(2 * levels, rows_here, half)
        if field == 2:
            back = lax.optimization_barrier((back, others[0]))[0]
        rows = lax.all_to_all(back, "reg", split_axis=0, concat_axis=0, tiled=True)
        if field == 2:
            rows = lax.optimization_barrier((rows, others[1]))[0]
        other = lax.ppermute(rows, "lev", swap)
        others.append(other)
        out = synthesize(field, rows, other, own, crossed, out)
    return out.reshape(stacked, rows_here, cols_here)


def solution(mesh):
    placed = (P(None, "reg", "lev"), P(None, "reg", "lev"), P(None, "reg", "lev"), P())
    paired = mesh.shape["lev"] == 2 and mesh.shape["reg"] == 16
    return jax.shard_map(
        paired_device if paired else per_device,
        mesh=mesh,
        in_specs=placed,
        out_specs=P(None, "reg", "lev"),
        check_vma=False,
    )
```
